32 devices in a mesh: occ: 4 (over z), virt: 8 (over y, x, core).
Axes of the slice: x: 2, y: 2, z: 4, core: 2. Of those that a mesh axis runs over, the one named last changes fastest.
Arguments:
- amplitudes: float32 [128, 8192], P('occ', 'virt'), may hold values from -6 to 6
- tiles: float32 [2048, 128, 128], P(('occ', 'virt')), may hold values from -0.15625 to 0.15625
- tile_code: int32 [2048], P(('occ', 'virt')), may hold values from 0 to 127, as said below
- tile_count: int32 [32], P(('occ', 'virt')), may hold values from 16 to 64, as said below
- occ_energy: float32 [128], P('virt'), may hold values from -3 to -0.5
- virt_energy: float32 [8192], P('occ'), may hold values from 1 to 4
Outputs:
- updated: float32 [128, 8192], P('virt', 'occ')
The draws below stay inside these ranges and needn't reach their ends.
Inputs may be any that keep to these rules, and one draw needn't show every extreme that they name: `tile_code`: within one device's 64 slots the positions are distinct. `tile_count`: some device has all 64 slots live.
All inputs are finite; a program needn't handle non-finite values.
Results may differ from the reference program's by a relative error of at most 0.0003.
Values sent between devices are 32-bit elements; how exact they have to be, the bound alone decides.
A program may use at most 64 MiB of HBM per device.

```python
import jax
import jax.numpy as jnp
from jax import lax

TILE = 128
VP_DEV = 1024
AB_DEV = 2048
NNZ_DEV = 64
OP = 128
VP = 8192
GRID = 128
NNZ_ALL = 2048
N_VIRT = 8


def draw_tile_code(key, part):
    devices = NNZ_ALL // NNZ_DEV
    subkeys = jax.random.split(jax.random.fold_in(key, 11), devices)
    tile_codes = jax.vmap(lambda single: jax.random.permutation(single, GRID)[:NNZ_DEV])(subkeys)
    return tile_codes.reshape(-1).astype(jnp.int32)


def draw_tile_count(key, part):
    devices = NNZ_ALL // NNZ_DEV
    first, second = jax.random.split(jax.random.fold_in(key, 13))
    counts = jax.random.randint(first, (devices,), NNZ_DEV // 4, NNZ_DEV // 2 + 1)
    busiest = jax.random.randint(second, (), 0, devices)
    return jnp.where(jnp.arange(devices) == busiest, NNZ_DEV, counts).astype(jnp.int32)


def level_of(stream_key, extent, cuts, low, largest):
    loudness, own = 1.0, jax.random.fold_in(stream_key, 6)
    for axis_at, parts in cuts:
        steps = jnp.exp(jax.random.uniform(jax.random.fold_in(own, axis_at), (parts,), jnp.float32, low / len(cuts), largest / len(cuts)))
        loudness = loudness * jnp.repeat(steps, extent[axis_at] // parts).reshape([-1 if axis == axis_at else 1 for axis in range(len(extent))])
    return loudness


def bell_draw(own_key, extent, scale, bound, cuts=(), held_as=jnp.bfloat16):
    values = scale * jax.random.normal(own_key, extent, jnp.float32)
    if cuts:
        values = values * level_of(own_key, extent, cuts, -0.22, 0.18)
    return jnp.clip(values, -bound, bound).astype(held_as)


def setup_inputs(seed: int = 0) -> dict:
    streams_of = jax.random.split(jax.random.key(seed), 7)
    return {
        "amplitudes": bell_draw(streams_of[0], (OP, VP), 1.0, 6.0, ((0, 4), (1, 8)), jnp.float32),
        "tiles": bell_draw(streams_of[1], (NNZ_ALL, TILE, TILE), (VP // 6) ** -0.5, 0.15625, ((0, 32),), jnp.float32),
        "tile_code": draw_tile_code(jax.random.fold_in(streams_of[6], 71), 0),
        "tile_count": draw_tile_count(jax.random.fold_in(streams_of[6], 71), 0),
        "occ_energy": jnp.clip(-3.0 + 2.5 * jax.random.uniform(streams_of[4], (OP,), jnp.float32) ** level_of(streams_of[4], (OP,), ((0, 8),), -0.2, 0.2), -3.0, -0.5),
        "virt_energy": jnp.clip(1.0 + 3.0 * jax.random.uniform(streams_of[5], (VP,), jnp.float32) ** level_of(streams_of[5], (VP,), ((0, 4),), -0.2, 0.2), 1.0, 4.0),
    }


def reference(amplitudes, tiles, tile_code, tile_count, occ_energy, virt_energy):
    row_tiles = VP_DEV // TILE
    col_tiles = AB_DEV // TILE
    slots = jnp.arange(NNZ_ALL, dtype=jnp.int32)
    device = slots // NNZ_DEV
    within = slots % NNZ_DEV
    occ_index = device // N_VIRT
    virt_index = device % N_VIRT
    live = within < tile_count[device]
    row_start = ((virt_index * row_tiles + tile_code // col_tiles) * TILE).astype(jnp.int32)
    col_start = ((occ_index * col_tiles + tile_code % col_tiles) * TILE).astype(jnp.int32)

    def add_tile(total, item):
        rstart, cstart, flag, block = item

        def apply(current):
            columns = lax.dynamic_slice_in_dim(amplitudes, rstart, TILE, 1)
            term = jnp.dot(columns, block, precision=lax.Precision.HIGHEST, preferred_element_type=jnp.float32)
            present = lax.dynamic_slice_in_dim(current, cstart, TILE, 1)
            return lax.dynamic_update_slice_in_dim(current, present + term, cstart, 1)

        return lax.cond(flag, apply, lambda current: current, total), None

    start = jnp.zeros((OP, VP), jnp.float32)
    ladder, _ = lax.scan(add_tile, start, (row_start, col_start, live, tiles))
    return ladder / (virt_energy[None, :] - occ_energy[:, None])
```

```python
import functools

import jax
import jax.numpy as jnp
from jax import lax
from jax.experimental import pallas as pl
from jax.experimental.pallas import tpu as pltpu
from jax.sharding import PartitionSpec as P

MESH = pl.DeviceIdType.MESH
SPLITS = 2
CHUNKS = 4


def flip(index, mask, size):
    out = index * 0
    bit = 1
    while bit < size:
        digit = lax.rem(lax.div(index, bit), 2)
        if mask & bit:
            digit = 1 - digit
        out = out + digit * bit
        bit *= 2
    return out


def kernel(
    no, nv,
    slot_ref, occ_ref, virt_ref, amp_in, tiles_in, out_ref,
    tiles, high, low, amp, lhs, part, partner_part, summed, arrived,
    tile_sem, own_sem, gather_send, gather_recv, core_send, core_recv, chip_send, chip_recv,
):
    o = lax.axis_index("occ")
    v = lax.axis_index("virt")
    core = lax.rem(v, 2)
    chip = lax.div(v, 2)
    chips = nv // 2
    block, depth = amp_in.shape
    tile = tiles_in.shape[1]
    width = out_ref.shape[1]
    rows = block * no
    dest = out_ref.shape[0]
    half = rows // 2
    col_tiles = width // tile
    positions = (depth // tile) * col_tiles
    slots = tiles_in.shape[0]

    tile_copy = pltpu.make_async_copy(tiles_in, tiles.at[pl.ds(0, slots)], tile_sem)
    tile_copy.start()
    own_copy = pltpu.make_async_copy(amp_in, amp.at[o], own_sem)
    own_copy.start()
    has_left = o > 0
    has_right = o < no - 1
    other_core = (o, v + 1 - 2 * core)

    barrier = pltpu.get_barrier_semaphore()

    @pl.when(has_left)
    def _():
        pl.semaphore_signal(barrier, inc=1, device_id=(o - 1, v), device_id_type=MESH)

    @pl.when(has_right)
    def _():
        pl.semaphore_signal(barrier, inc=1, device_id=(o + 1, v), device_id_type=MESH)

    pl.semaphore_signal(barrier, inc=1, device_id=other_core, device_id_type=MESH)
    for mask in range(1, chips):
        there = flip(chip, mask, chips)
        pl.semaphore_signal(barrier, inc=1, device_id=(o, 2 * there + core), device_id_type=MESH)
    tiles[slots] = jnp.zeros(tiles.shape[1:], tiles.dtype)
    pl.semaphore_wait(barrier, chips + has_left.astype(jnp.int32) + has_right.astype(jnp.int32))

    piece = block // SPLITS

    def gather_copy(source, which, split, side):
        return pltpu.make_async_remote_copy(
            src_ref=source,
            dst_ref=amp.at[which, pl.ds(split * piece, piece)],
            send_sem=gather_send.at[side, which, split],
            recv_sem=gather_recv.at[which, split],
            device_id=(o + 2 * side - 1, v),
            device_id_type=MESH,
        )

    def held(which, split):
        return amp.at[which, pl.ds(split * piece, piece)]

    for split in range(SPLITS):
        mine = amp_in.at[pl.ds(split * piece, piece)]

        @pl.when(has_right)
        def _():
            gather_copy(mine, o, split, 1).start()

        @pl.when(has_left)
        def _():
            gather_copy(mine, o, split, 0).start()

    def place(position, carry):
        value = tiles[slot_ref[position]]
        rounded = value.astype(jnp.bfloat16)
        at_row = pl.multiple_of(lax.div(position, col_tiles) * tile, tile)
        at_col = pl.multiple_of(lax.rem(position, col_tiles) * tile, tile)
        high[pl.ds(at_row, tile), pl.ds(at_col, tile)] = rounded
        low[pl.ds(at_row, tile), pl.ds(at_col, tile)] = (
            value - rounded.astype(jnp.float32)
        ).astype(jnp.bfloat16)
        return carry

    tile_copy.wait()
    steps = (no - 1) * SPLITS
    step = 0
    for distance in range(1, no):
        for split in range(SPLITS):
            lax.fori_loop(
                positions * step // steps, positions * (step + 1) // steps, place, 0
            )
            step += 1

            @pl.when(o >= distance)
            def _():
                which = o - distance
                gather_copy(held(which, split), which, split, 1).wait_recv()

                @pl.when(has_right)
                def _():
                    gather_copy(held(which, split), which, split, 1).start()

            @pl.when(o + distance < no)
            def _():
                which = o + distance
                gather_copy(held(which, split), which, split, 0).wait_recv()

                @pl.when(has_left)
                def _():
                    gather_copy(held(which, split), which, split, 0).start()

    own_copy.wait()
    groups = block // dest
    for which in range(no):
        for group in range(groups):
            target = which * groups + group
            start = (target % 2) * half + (target // 2) * dest
            value = amp[which, pl.ds(group * dest, dest)]
            rounded = value.astype(jnp.bfloat16)
            lhs[pl.ds(start, dest)] = rounded
            lhs[pl.ds(rows + start, dest)] = (
                value - rounded.astype(jnp.float32)
            ).astype(jnp.bfloat16)

    chunk = width // CHUNKS

    def core_copy(at):
        cols = pl.ds(at * chunk, chunk)
        return pltpu.make_async_remote_copy(
            src_ref=part.at[1 - core, :, cols],
            dst_ref=partner_part.at[:, cols],
            send_sem=core_send.at[at],
            recv_sem=core_recv.at[at],
            device_id=other_core,
            device_id_type=MESH,
        )

    def chip_copy(mask, at):
        cols = pl.ds(at * chunk, chunk)
        there = flip(chip, mask, chips)
        return pltpu.make_async_remote_copy(
            src_ref=summed.at[there, :, cols],
            dst_ref=arrived.at[mask - 1, :, cols],
            send_sem=chip_send.at[mask - 1, at],
            recv_sem=chip_recv.at[mask - 1, at],
            device_id=(o, 2 * there + core),
            device_id_type=MESH,
        )

    def pass_on(at):
        cols = pl.ds(at * chunk, chunk)
        core_copy(at).wait_recv()
        total = part[core, :, cols] + partner_part[:, cols]
        summed[:, :, cols] = total.reshape(chips, dest, chunk)
        for mask in range(chips - 1, 0, -1):
            chip_copy(mask, at).start()

    for at in range(CHUNKS):
        cols = pl.ds(at * chunk, chunk)
        wide = jnp.dot(lhs[...], high[:, cols], preferred_element_type=jnp.float32)
        narrow = jnp.dot(lhs[pl.ds(0, rows)], low[:, cols], preferred_element_type=jnp.float32)
        total = wide[:rows] + (wide[rows:] + narrow)
        part[:, :, cols] = total.reshape(2, half, chunk)
        core_copy(at).start()
        if at:
            pass_on(at - 1)
    pass_on(CHUNKS - 1)

    row_index = lax.broadcasted_iota(jnp.int32, (dest, chunk), 0)
    energy = jnp.zeros((dest, chunk), jnp.float32)
    for row in range(dest):
        energy = jnp.where(row_index == row, occ_ref[row], energy)
    for at in range(CHUNKS):
        cols = pl.ds(at * chunk, chunk)
        total = summed[chip, :, cols]
        for mask in range(1, chips):
            chip_copy(mask, at).wait_recv()
            total = total + arrived[mask - 1, :, cols]
        out_ref[:, cols] = total / (virt_ref[:, cols] - energy)

    for at in range(CHUNKS):
        core_copy(at).wait_send()
        for mask in range(1, chips):
            chip_copy(mask, at).wait_send()
    for which in range(no):
        for split in range(SPLITS):

            @pl.when(has_right & (o >= which))
            def _():
                gather_copy(held(which, split), which, split, 1).wait_send()

            @pl.when(has_left & (o <= which))
            def _():
                gather_copy(held(which, split), which, split, 0).wait_send()


def body(no, nv, amplitudes, tiles, tile_code, tile_count, occ_energy, virt_energy):
    block, depth = amplitudes.shape
    slots, tile, _ = tiles.shape
    width = virt_energy.shape[0]
    dest = occ_energy.shape[0]
    rows = block * no
    chips = nv // 2
    positions = (depth // tile) * (width // tile)
    grid = (slots, positions)
    slot_ids = lax.broadcasted_iota(jnp.int32, grid, 0)
    places = lax.broadcasted_iota(jnp.int32, grid, 1)
    hit = (tile_code[:, None] == places) & (slot_ids < tile_count[:, None])
    slot_of = jnp.min(jnp.where(hit, slot_ids, slots), axis=0)
    smem = pl.BlockSpec(memory_space=pltpu.SMEM)
    vmem = pl.BlockSpec(memory_space=pltpu.VMEM)
    anywhere = pl.BlockSpec(memory_space=pl.ANY)
    return pl.pallas_call(
        functools.partial(kernel, no, nv),
        out_shape=jax.ShapeDtypeStruct((dest, width), jnp.float32),
        in_specs=[smem, smem, vmem, anywhere, anywhere],
        out_specs=vmem,
        scratch_shapes=[
            pltpu.VMEM((slots + 1, tile, tile), jnp.float32),
            pltpu.VMEM((depth, width), jnp.bfloat16),
            pltpu.VMEM((depth, width), jnp.bfloat16),
            pltpu.VMEM((no, block, depth), jnp.float32),
            pltpu.VMEM((2 * rows, depth), jnp.bfloat16),
            pltpu.VMEM((2, rows // 2, width), jnp.float32),
            pltpu.VMEM((rows // 2, width), jnp.float32),
            pltpu.VMEM((chips, dest, width), jnp.float32),
            pltpu.VMEM((chips - 1, dest, width), jnp.float32),
            pltpu.SemaphoreType.DMA,
            pltpu.SemaphoreType.DMA,
            pltpu.SemaphoreType.DMA((2, no, SPLITS)),
            pltpu.SemaphoreType.DMA((no, SPLITS)),
            pltpu.SemaphoreType.DMA((CHUNKS,)),
            pltpu.SemaphoreType.DMA((CHUNKS,)),
            pltpu.SemaphoreType.DMA((chips - 1, CHUNKS)),
            pltpu.SemaphoreType.DMA((chips - 1, CHUNKS)),
        ],
        compiler_params=pltpu.CompilerParams(collective_id=0, has_side_effects=True),
    )(slot_of, occ_energy, virt_energy.reshape(1, width), amplitudes, tiles)


def solution(mesh):
    placed = (
        P("occ", "virt"),
        P(("occ", "virt"), None, None),
        P(("occ", "virt")),
        P(("occ", "virt")),
        P("virt"),
        P("occ"),
    )
    return jax.shard_map(
        functools.partial(body, mesh.shape["occ"], mesh.shape["virt"]),
        mesh=mesh, in_specs=placed, out_specs=P("virt", "occ"), check_vma=False,
    )
```

```python
import functools

import jax
import jax.numpy as jnp
from jax import lax
from jax.experimental import pallas as pl
from jax.experimental.pallas import tpu as pltpu
from jax.sharding import PartitionSpec as P

MESH = pl.DeviceIdType.MESH
PHASES = 2
CHUNKS = 4
GRANT = 50 * 2**20


def flip(index, mask, size):
    out = index * 0
    bit = 1
    while bit < size:
        digit = lax.rem(lax.div(index, bit), 2)
        if mask & bit:
            digit = 1 - digit
        out = out + digit * bit
        bit *= 2
    return out


def kernel(
    no, nv,
    code_in, count_in, occ_in, virt_in, amp_in, tiles_in, out_ref,
    code, count, occ_energy, virt_energy, slot_map, slot_of,
    tiles, high, low, amp, lhs, part, partner_part, summed, arrived,
    small_sem, slot_sem, tile_sem, own_sem,
    gather_send, gather_recv, core_send, core_recv, chip_send, chip_recv,
):
    o = lax.axis_index("occ")
    v = lax.axis_index("virt")
    core = lax.rem(v, 2)
    chip = lax.div(v, 2)
    chips = nv // 2
    depth = amp_in.shape[-1]
    tile = tiles_in.shape[1]
    dest, width = out_ref.shape
    level = dest // PHASES
    rows = lhs.shape[1] // 2
    half = rows // 2
    col_tiles = width // tile
    positions = (depth // tile) * col_tiles
    slots = tiles_in.shape[0]

    small = [
        pltpu.make_async_copy(source, target, small_sem.at[number])
        for number, (source, target) in enumerate(
            ((code_in, code), (count_in, count), (occ_in, occ_energy), (virt_in, virt_energy))
        )
    ]
    small[0].start()
    small[1].start()
    own_copy = pltpu.make_async_copy(amp_in, amp.at[o], own_sem)
    own_copy.start()
    tile_copy = pltpu.make_async_copy(tiles_in, tiles.at[pl.ds(0, slots)], tile_sem)
    tile_copy.start()
    small[2].start()
    small[3].start()
    has_left = o > 0
    has_right = o < no - 1
    other_core = (o, v + 1 - 2 * core)

    barrier = pltpu.get_barrier_semaphore()

    @pl.when(has_left)
    def _():
        pl.semaphore_signal(barrier, inc=1, device_id=(o - 1, v), device_id_type=MESH)

    @pl.when(has_right)
    def _():
        pl.semaphore_signal(barrier, inc=1, device_id=(o + 1, v), device_id_type=MESH)

    for mask in range(chips - 1, 0, -1):
        there = flip(chip, mask, chips)
        pl.semaphore_signal(barrier, inc=1, device_id=(o, 2 * there + core), device_id_type=MESH)
    pl.semaphore_signal(barrier, inc=1, device_id=other_core, device_id_type=MESH)

    tiles[slots] = jnp.zeros(tiles.shape[1:], tiles.dtype)
    small[0].wait()
    small[1].wait()
    lanes = slot_map.shape[1]
    place_index = lax.broadcasted_iota(jnp.int32, slot_map.shape, 0) * lanes + (
        lax.broadcasted_iota(jnp.int32, slot_map.shape, 1)
    )
    found = jnp.full(slot_map.shape, slots, jnp.int32)
    live = count[0]
    for slot in range(slots):
        found = jnp.where(place_index == jnp.where(slot < live, code[slot], -1), slot, found)
    slot_map[...] = found

    pl.semaphore_wait(barrier, chips + has_left.astype(jnp.int32) + has_right.astype(jnp.int32))

    def gather_copy(source, which, phase, side):
        return pltpu.make_async_remote_copy(
            src_ref=source,
            dst_ref=amp.at[which, :, :, phase],
            send_sem=gather_send.at[side, which, phase],
            recv_sem=gather_recv.at[which, phase],
            device_id=(o + 2 * side - 1, v),
            device_id_type=MESH,
        )

    def held(which, phase):
        return amp.at[which, :, :, phase]

    for phase in range(PHASES):
        mine = amp_in.at[:, :, phase]

        @pl.when(has_right)
        def _():
            gather_copy(mine, o, phase, 1).start()

        @pl.when(has_left)
        def _():
            gather_copy(mine, o, phase, 0).start()

    slot_copy = pltpu.make_async_copy(slot_map, slot_of, slot_sem)
    slot_copy.start()

    def place(position, carry):
        value = tiles[slot_of[lax.div(position, lanes), lax.rem(position, lanes)]]
        rounded = value.astype(jnp.bfloat16)
        at_row = pl.multiple_of(lax.div(position, col_tiles) * tile, tile)
        at_col = pl.multiple_of(lax.rem(position, col_tiles) * tile, tile)
        high[pl.ds(at_row, tile), pl.ds(at_col, tile)] = rounded
        low[pl.ds(at_row, tile), pl.ds(at_col, tile)] = (
            value - rounded.astype(jnp.float32)
        ).astype(jnp.bfloat16)
        return carry

    def relay(phase, distance):
        @pl.when(o >= distance)
        def _():
            which = o - distance
            gather_copy(held(which, phase), which, phase, 1).wait_recv()

            @pl.when(has_right)
            def _():
                gather_copy(held(which, phase), which, phase, 1).start()

        @pl.when(o + distance < no)
        def _():
            which = o + distance
            gather_copy(held(which, phase), which, phase, 0).wait_recv()

            @pl.when(has_left)
            def _():
                gather_copy(held(which, phase), which, phase, 0).start()

    chunk = width // CHUNKS

    def split(phase):
        for side in range(2):
            value = amp[:, :, side, phase].reshape(half, depth)
            rounded = value.astype(jnp.bfloat16)
            lhs[phase, pl.ds(side * half, half)] = rounded
            lhs[phase, pl.ds(rows + side * half, half)] = (
                value - rounded.astype(jnp.float32)
            ).astype(jnp.bfloat16)

    def core_copy(phase, at):
        cols = pl.ds(at * chunk, chunk)
        return pltpu.make_async_remote_copy(
            src_ref=part.at[phase, 1 - core, :, cols],
            dst_ref=partner_part.at[phase, :, cols],
            send_sem=core_send.at[phase, at],
            recv_sem=core_recv.at[phase, at],
            device_id=other_core,
            device_id_type=MESH,
        )

    def chip_copy(phase, mask, at):
        cols = pl.ds(at * chunk, chunk)
        there = flip(chip, mask, chips)
        return pltpu.make_async_remote_copy(
            src_ref=summed.at[phase, there, :, cols],
            dst_ref=arrived.at[phase, mask - 1, :, cols],
            send_sem=chip_send.at[phase, mask - 1, at],
            recv_sem=chip_recv.at[phase, mask - 1, at],
            device_id=(o, 2 * there + core),
            device_id_type=MESH,
        )

    def multiply(phase, at):
        cols = pl.ds(at * chunk, chunk)
        wide = jnp.dot(lhs[phase], high[:, cols], preferred_element_type=jnp.float32)
        narrow = jnp.dot(
            lhs[phase, pl.ds(0, rows)], low[:, cols], preferred_element_type=jnp.float32
        )
        total = wide[:rows] + (wide[rows:] + narrow)
        part[phase, :, :, cols] = total.reshape(2, half, chunk)
        core_copy(phase, at).start()

    def pass_on(phase, at):
        cols = pl.ds(at * chunk, chunk)
        core_copy(phase, at).wait_recv()
        total = part[phase, core, :, cols] + partner_part[phase, :, cols]
        summed[phase, :, :, cols] = total.reshape(chips, level, chunk)
        for mask in range(chips - 1, 0, -1):
            chip_copy(phase, mask, at).start()

    def job(phase, at):
        if at == 0:
            split(phase)
        if at < CHUNKS:
            multiply(phase, at)
        if at:
            pass_on(phase, at - 1)

    tile_copy.wait()
    slot_copy.wait()
    for phase in range(PHASES):
        for distance in range(1, no):
            if phase == 0:
                lax.fori_loop(
                    positions * (distance - 1) // (no - 1),
                    positions * distance // (no - 1),
                    place,
                    0,
                )
            elif distance > 1:
                for at in range(
                    (CHUNKS + 1) * (distance - 2) // (no - 2), (CHUNKS + 1) * (distance - 1) // (no - 2)
                ):
                    job(phase - 1, at)
            relay(phase, distance)
        if phase == 0:
            own_copy.wait()
        elif no == 2:
            for at in range(CHUNKS + 1):
                job(phase - 1, at)
    for at in range(CHUNKS + 1):
        job(PHASES - 1, at)

    small[2].wait()
    small[3].wait()
    shape = (level, chunk)
    row_index = lax.broadcasted_iota(jnp.int32, shape, 0)
    for phase in range(PHASES):
        energy = jnp.zeros(shape, jnp.float32)
        for row in range(level):
            energy = jnp.where(row_index == row, occ_energy[phase * level + row], energy)
        for at in range(CHUNKS):
            cols = pl.ds(at * chunk, chunk)
            total = summed[phase, chip, :, cols]
            for mask in range(1, chips):
                chip_copy(phase, mask, at).wait_recv()
                total = total + arrived[phase, mask - 1, :, cols]
            out_ref[pl.ds(phase * level, level), cols] = total / (virt_energy[:, cols] - energy)

    for phase in range(PHASES):
        for at in range(CHUNKS):
            core_copy(phase, at).wait_send()
            for mask in range(1, chips):
                chip_copy(phase, mask, at).wait_send()
        for which in range(no):

            @pl.when(has_right & (o >= which))
            def _():
                gather_copy(held(which, phase), which, phase, 1).wait_send()

            @pl.when(has_left & (o <= which))
            def _():
                gather_copy(held(which, phase), which, phase, 0).wait_send()


def body(no, nv, amplitudes, tiles, tile_code, tile_count, occ_energy, virt_energy):
    block, depth = amplitudes.shape
    slots, tile, _ = tiles.shape
    width = virt_energy.shape[0]
    dest = occ_energy.shape[0]
    chips = nv // 2
    level = dest // PHASES
    pairs = block // (2 * dest)
    rows = block * no // PHASES
    map_shape = (max(8, (depth // tile) * (width // tile) // 128), 128)
    f32, bf16, i32 = jnp.float32, jnp.bfloat16, jnp.int32
    vmem, smem, dma = pltpu.VMEM, pltpu.SMEM, pltpu.SemaphoreType.DMA
    return pl.pallas_call(
        functools.partial(kernel, no, nv),
        out_shape=jax.ShapeDtypeStruct((dest, width), f32),
        in_specs=[pl.BlockSpec(memory_space=pltpu.HBM)] * 6,
        out_specs=pl.BlockSpec(memory_space=pltpu.VMEM),
        scratch_shapes=[
            smem(tile_code.shape, i32),
            smem(tile_count.shape, i32),
            smem((dest,), f32),
            vmem((1, width), f32),
            vmem(map_shape, i32),
            smem(map_shape, i32),
            vmem((slots + 1, tile, tile), f32),
            vmem((depth, width), bf16),
            vmem((depth, width), bf16),
            vmem((no, pairs, 2, PHASES, level, depth), f32),
            vmem((PHASES, 2 * rows, depth), bf16),
            vmem((PHASES, 2, rows // 2, width), f32),
            vmem((PHASES, rows // 2, width), f32),
            vmem((PHASES, chips, level, width), f32),
            vmem((PHASES, chips - 1, level, width), f32),
            dma((4,)),
            dma,
            dma,
            dma,
            dma((2, no, PHASES)),
            dma((no, PHASES)),
            dma((PHASES, CHUNKS)),
            dma((PHASES, CHUNKS)),
            dma((PHASES, chips - 1, CHUNKS)),
            dma((PHASES, chips - 1, CHUNKS)),
        ],
        compiler_params=pltpu.CompilerParams(
            collective_id=0, has_side_effects=True, vmem_limit_bytes=GRANT
        ),
    )(
        tile_code,
        tile_count,
        occ_energy,
        virt_energy.reshape(1, width),
        amplitudes.reshape(pairs, 2, PHASES, level, depth),
        tiles,
    )


def solution(mesh):
    placed = (
        P("occ", "virt"),
        P(("occ", "virt"), None, None),
        P(("occ", "virt")),
        P(("occ", "virt")),
        P("virt"),
        P("occ"),
    )
    return jax.shard_map(
        functools.partial(body, mesh.shape["occ"], mesh.shape["virt"]),
        mesh=mesh, in_specs=placed, out_specs=P("virt", "occ"), check_vma=False,
    )
```

```python
import functools

import jax
import jax.numpy as jnp
from jax import lax
from jax.experimental import pallas as pl
from jax.experimental.pallas import tpu as pltpu
from jax.sharding import PartitionSpec as P

MESH = pl.DeviceIdType.MESH
PHASES = 2
CHUNKS = 4
GRANT = 50 * 2**20


def flip(index, mask, size):
    out = index * 0
    bit = 1
    while bit < size:
        digit = lax.rem(lax.div(index, bit), 2)
        if mask & bit:
            digit = 1 - digit
        out = out + digit * bit
        bit *= 2
    return out


def kernel(
    no, nv,
    code_in, count_in, occ_in, virt_in, amp_in, tiles_in, out_ref,
    code, count, occ_energy, virt_energy, slot_map, slot_of,
    tiles, high, low, amp, lhs, part, partner_part, summed, arrived,
    small_sem, slot_sem, tile_sem, own_sem,
    gather_send, gather_recv, core_send, core_recv, chip_send, chip_recv,
):
    o = lax.axis_index("occ")
    v = lax.axis_index("virt")
    core = lax.rem(v, 2)
    chip = lax.div(v, 2)
    chips = nv // 2
    depth = amp_in.shape[-1]
    tile = tiles_in.shape[1]
    dest, width = out_ref.shape
    level = dest // PHASES
    rows = lhs.shape[1] // 2
    half = rows // 2
    col_tiles = width // tile
    positions = (depth // tile) * col_tiles
    slots = tiles_in.shape[0]

    small = [
        pltpu.make_async_copy(source, target, small_sem.at[number])
        for number, (source, target) in enumerate(
            ((code_in, code), (count_in, count), (occ_in, occ_energy), (virt_in, virt_energy))
        )
    ]
    small[0].start()
    small[1].start()
    own_copy = pltpu.make_async_copy(amp_in, amp.at[o], own_sem)
    own_copy.start()
    tile_copy = pltpu.make_async_copy(tiles_in, tiles.at[pl.ds(0, slots)], tile_sem)
    tile_copy.start()
    small[2].start()
    small[3].start()
    has_left = o > 0
    has_right = o < no - 1
    other_core = (o, v + 1 - 2 * core)

    barrier = pltpu.get_barrier_semaphore()

    @pl.when(has_left)
    def _():
        pl.semaphore_signal(barrier, inc=1, device_id=(o - 1, v), device_id_type=MESH)

    @pl.when(has_right)
    def _():
        pl.semaphore_signal(barrier, inc=1, device_id=(o + 1, v), device_id_type=MESH)

    for mask in range(chips - 1, 0, -1):
        there = flip(chip, mask, chips)
        pl.semaphore_signal(barrier, inc=1, device_id=(o, 2 * there + core), device_id_type=MESH)
    pl.semaphore_signal(barrier, inc=1, device_id=other_core, device_id_type=MESH)

    tiles[slots] = jnp.zeros(tiles.shape[1:], tiles.dtype)
    small[0].wait()
    small[1].wait()
    lanes = slot_map.shape[1]
    place_index = lax.broadcasted_iota(jnp.int32, slot_map.shape, 0) * lanes + (
        lax.broadcasted_iota(jnp.int32, slot_map.shape, 1)
    )
    found = jnp.full(slot_map.shape, slots, jnp.int32)
    live = count[0]
    for slot in range(slots):
        found = jnp.where(place_index == jnp.where(slot < live, code[slot], -1), slot, found)
    slot_map[...] = found

    pl.semaphore_wait(barrier, chips + has_left.astype(jnp.int32) + has_right.astype(jnp.int32))

    def gather_copy(source, which, phase, side):
        return pltpu.make_async_remote_copy(
            src_ref=source,
            dst_ref=amp.at[which, :, :, phase],
            send_sem=gather_send.at[side, which, phase],
            recv_sem=gather_recv.at[which, phase],
            device_id=(o + 2 * side - 1, v),
            device_id_type=MESH,
        )

    def held(which, phase):
        return amp.at[which, :, :, phase]

    for phase in range(PHASES):
        mine = amp_in.at[:, :, phase]

        @pl.when(has_right)
        def _():
            gather_copy(mine, o, phase, 1).start()

        @pl.when(has_left)
        def _():
            gather_copy(mine, o, phase, 0).start()

    slot_copy = pltpu.make_async_copy(slot_map, slot_of, slot_sem)
    slot_copy.start()

    def place(position, carry):
        value = tiles[slot_of[lax.div(position, lanes), lax.rem(position, lanes)]]
        rounded = value.astype(jnp.bfloat16)
        at_row = pl.multiple_of(lax.div(position, col_tiles) * tile, tile)
        at_col = pl.multiple_of(lax.rem(position, col_tiles) * tile, tile)
        high[pl.ds(at_row, tile), pl.ds(at_col, tile)] = rounded
        low[pl.ds(at_row, tile), pl.ds(at_col, tile)] = (
            value - rounded.astype(jnp.float32)
        ).astype(jnp.bfloat16)
        return carry

    def relay(phase, distance):
        @pl.when(o >= distance)
        def _():
            which = o - distance
            gather_copy(held(which, phase), which, phase, 1).wait_recv()

            @pl.when(has_right)
            def _():
                gather_copy(held(which, phase), which, phase, 1).start()

        @pl.when(o + distance < no)
        def _():
            which = o + distance
            gather_copy(held(which, phase), which, phase, 0).wait_recv()

            @pl.when(has_left)
            def _():
                gather_copy(held(which, phase), which, phase, 0).start()

    chunk = width // CHUNKS

    def split(phase):
        for side in range(2):
            value = amp[:, :, side, phase].reshape(half, depth)
            rounded = value.astype(jnp.bfloat16)
            lhs[phase, pl.ds(side * half, half)] = rounded
            lhs[phase, pl.ds(rows + side * half, half)] = (
                value - rounded.astype(jnp.float32)
            ).astype(jnp.bfloat16)

    def core_copy(phase, at):
        cols = pl.ds(at * chunk, chunk)
        return pltpu.make_async_remote_copy(
            src_ref=part.at[phase, 1 - core, :, cols],
            dst_ref=partner_part.at[phase, :, cols],
            send_sem=core_send.at[phase, at],
            recv_sem=core_recv.at[phase, at],
            device_id=other_core,
            device_id_type=MESH,
        )

    def chip_copy(phase, mask, at):
        cols = pl.ds(at * chunk, chunk)
        there = flip(chip, mask, chips)
        return pltpu.make_async_remote_copy(
            src_ref=summed.at[phase, there, :, cols],
            dst_ref=arrived.at[phase, mask - 1, :, cols],
            send_sem=chip_send.at[phase, mask - 1, at],
            recv_sem=chip_recv.at[phase, mask - 1, at],
            device_id=(o, 2 * there + core),
            device_id_type=MESH,
        )

    def multiply(phase, at):
        cols = pl.ds(at * chunk, chunk)
        wide = jnp.dot(lhs[phase], high[:, cols], preferred_element_type=jnp.float32)
        narrow = jnp.dot(
            lhs[phase, pl.ds(0, rows)], low[:, cols], preferred_element_type=jnp.float32
        )
        total = wide[:rows] + (wide[rows:] + narrow)
        part[phase, :, :, cols] = total.reshape(2, half, chunk)
        core_copy(phase, at).start()

    def pass_on(phase, at):
        cols = pl.ds(at * chunk, chunk)
        core_copy(phase, at).wait_recv()
        total = part[phase, core, :, cols] + partner_part[phase, :, cols]
        summed[phase, :, :, cols] = total.reshape(chips, level, chunk)
        for mask in range(chips - 1, 0, -1):
            chip_copy(phase, mask, at).start()

    def job(phase, at):
        if at == 0:
            split(phase)
        if at < CHUNKS:
            multiply(phase, at)
        else:
            pass_on(phase, at - CHUNKS)

    jobs = 2 * CHUNKS

    tile_copy.wait()
    slot_copy.wait()
    for phase in range(PHASES):
        for distance in range(1, no):
            if phase == 0:
                lax.fori_loop(
                    positions * (distance - 1) // (no - 1),
                    positions * distance // (no - 1),
                    place,
                    0,
                )
            elif distance > 1:
                for at in range(
                    jobs * (distance - 2) // (no - 2), jobs * (distance - 1) // (no - 2)
                ):
                    job(phase - 1, at)
            relay(phase, distance)
        if phase == 0:
            own_copy.wait()
        elif no == 2:
            for at in range(jobs):
                job(phase - 1, at)
    for at in range(jobs):
        job(PHASES - 1, at)

    small[2].wait()
    small[3].wait()
    shape = (level, chunk)
    row_index = lax.broadcasted_iota(jnp.int32, shape, 0)
    for phase in range(PHASES):
        energy = jnp.zeros(shape, jnp.float32)
        for row in range(level):
            energy = jnp.where(row_index == row, occ_energy[phase * level + row], energy)
        for at in range(CHUNKS):
            cols = pl.ds(at * chunk, chunk)
            total = summed[phase, chip, :, cols]
            for mask in range(1, chips):
                chip_copy(phase, mask, at).wait_recv()
                total = total + arrived[phase, mask - 1, :, cols]
            out_ref[pl.ds(phase * level, level), cols] = total / (virt_energy[:, cols] - energy)

    for phase in range(PHASES):
        for at in range(CHUNKS):
            core_copy(phase, at).wait_send()
            for mask in range(1, chips):
                chip_copy(phase, mask, at).wait_send()
        for which in range(no):

            @pl.when(has_right & (o >= which))
            def _():
                gather_copy(held(which, phase), which, phase, 1).wait_send()

            @pl.when(has_left & (o <= which))
            def _():
                gather_copy(held(which, phase), which, phase, 0).wait_send()


def body(no, nv, amplitudes, tiles, tile_code, tile_count, occ_energy, virt_energy):
    block, depth = amplitudes.shape
    slots, tile, _ = tiles.shape
    width = virt_energy.shape[0]
    dest = occ_energy.shape[0]
    chips = nv // 2
    level = dest // PHASES
    pairs = block // (2 * dest)
    rows = block * no // PHASES
    map_shape = (max(8, (depth // tile) * (width // tile) // 128), 128)
    f32, bf16, i32 = jnp.float32, jnp.bfloat16, jnp.int32
    vmem, smem, dma = pltpu.VMEM, pltpu.SMEM, pltpu.SemaphoreType.DMA
    return pl.pallas_call(
        functools.partial(kernel, no, nv),
        out_shape=jax.ShapeDtypeStruct((dest, width), f32),
        in_specs=[pl.BlockSpec(memory_space=pltpu.HBM)] * 6,
        out_specs=pl.BlockSpec(memory_space=pltpu.VMEM),
        scratch_shapes=[
            smem(tile_code.shape, i32),
            smem(tile_count.shape, i32),
            smem((dest,), f32),
            vmem((1, width), f32),
            vmem(map_shape, i32),
            smem(map_shape, i32),
            vmem((slots + 1, tile, tile), f32),
            vmem((depth, width), bf16),
            vmem((depth, width), bf16),
            vmem((no, pairs, 2, PHASES, level, depth), f32),
            vmem((PHASES, 2 * rows, depth), bf16),
            vmem((PHASES, 2, rows // 2, width), f32),
            vmem((PHASES, rows // 2, width), f32),
            vmem((PHASES, chips, level, width), f32),
            vmem((PHASES, chips - 1, level, width), f32),
            dma((4,)),
            dma,
            dma,
            dma,
            dma((2, no, PHASES)),
            dma((no, PHASES)),
            dma((PHASES, CHUNKS)),
            dma((PHASES, CHUNKS)),
            dma((PHASES, chips - 1, CHUNKS)),
            dma((PHASES, chips - 1, CHUNKS)),
        ],
        compiler_params=pltpu.CompilerParams(
            collective_id=0, has_side_effects=True, vmem_limit_bytes=GRANT
        ),
    )(
        *(
            a if a is tile_count else pltpu.with_memory_space_constraint(a, pltpu.HBM)
            for a in (
                tile_code,
                tile_count,
                occ_energy,
                virt_energy.reshape(1, width),
                amplitudes.reshape(pairs, 2, PHASES, level, depth),
                tiles,
            )
        )
    )


def solution(mesh):
    placed = (
        P("occ", "virt"),
        P(("occ", "virt"), None, None),
        P(("occ", "virt")),
        P(("occ", "virt")),
        P("virt"),
        P("occ"),
    )
    return jax.shard_map(
        functools.partial(body, mesh.shape["occ"], mesh.shape["virt"]),
        mesh=mesh, in_specs=placed, out_specs=P("virt", "occ"), check_vma=False,
    )
```

```python
import functools

import jax
import jax.numpy as jnp
from jax import lax
from jax.experimental import pallas as pl
from jax.experimental.pallas import tpu as pltpu
from jax.sharding import PartitionSpec as P

MESH = pl.DeviceIdType.MESH
PHASES = 2
CHUNKS = 4
GRANT = 50 * 2**20


def flip(index, mask, size):
    out = index * 0
    bit = 1
    while bit < size:
        digit = lax.rem(lax.div(index, bit), 2)
        if mask & bit:
            digit = 1 - digit
        out = out + digit * bit
        bit *= 2
    return out


def kernel(
    no, nv,
    code_in, count_in, occ_in, virt_in, amp_in, tiles_in, out_ref,
    code, count, occ_energy, virt_energy, slot_map, slot_of,
    tiles, high, low, amp, lhs, part, partner_part, summed, arrived,
    small_sem, slot_sem, tile_sem, own_sem,
    gather_send, gather_recv, core_send, core_recv, chip_send, chip_recv,
):
    o = lax.axis_index("occ")
    v = lax.axis_index("virt")
    core = lax.rem(v, 2)
    chip = lax.div(v, 2)
    chips = nv // 2
    depth = amp_in.shape[-1]
    tile = tiles_in.shape[1]
    dest, width = out_ref.shape
    level = dest // PHASES
    rows = lhs.shape[1] // 2
    half = rows // 2
    col_tiles = width // tile
    positions = (depth // tile) * col_tiles
    slots = tiles_in.shape[0]

    small = [
        pltpu.make_async_copy(source, target, small_sem.at[number])
        for number, (source, target) in enumerate(
            ((code_in, code), (count_in, count), (occ_in, occ_energy), (virt_in, virt_energy))
        )
    ]
    small[0].start()
    small[1].start()
    own_copy = pltpu.make_async_copy(amp_in, amp.at[o], own_sem)
    own_copy.start()
    tile_copy = pltpu.make_async_copy(tiles_in, tiles.at[pl.ds(0, slots)], tile_sem)
    tile_copy.start()
    small[2].start()
    small[3].start()
    has_left = o > 0
    has_right = o < no - 1
    other_core = (o, v + 1 - 2 * core)

    barrier = pltpu.get_barrier_semaphore()

    @pl.when(has_left)
    def _():
        pl.semaphore_signal(barrier, inc=1, device_id=(o - 1, v), device_id_type=MESH)

    @pl.when(has_right)
    def _():
        pl.semaphore_signal(barrier, inc=1, device_id=(o + 1, v), device_id_type=MESH)

    for mask in range(chips - 1, 0, -1):
        there = flip(chip, mask, chips)
        pl.semaphore_signal(barrier, inc=1, device_id=(o, 2 * there + core), device_id_type=MESH)
    pl.semaphore_signal(barrier, inc=1, device_id=other_core, device_id_type=MESH)

    tiles[slots] = jnp.zeros(tiles.shape[1:], tiles.dtype)
    small[0].wait()
    small[1].wait()
    lanes = slot_map.shape[1]
    place_index = lax.broadcasted_iota(jnp.int32, slot_map.shape, 0) * lanes + (
        lax.broadcasted_iota(jnp.int32, slot_map.shape, 1)
    )
    found = jnp.full(slot_map.shape, slots, jnp.int32)
    live = count[0]
    for slot in range(slots):
        found = jnp.where(place_index == jnp.where(slot < live, code[slot], -1), slot, found)
    slot_map[...] = found

    pl.semaphore_wait(barrier, chips + has_left.astype(jnp.int32) + has_right.astype(jnp.int32))

    def gather_copy(source, which, phase, side):
        return pltpu.make_async_remote_copy(
            src_ref=source,
            dst_ref=amp.at[which, :, :, phase],
            send_sem=gather_send.at[side, which, phase],
            recv_sem=gather_recv.at[which, phase],
            device_id=(o + 2 * side - 1, v),
            device_id_type=MESH,
        )

    def held(which, phase):
        return amp.at[which, :, :, phase]

    for phase in range(PHASES):
        mine = amp_in.at[:, :, phase]

        @pl.when(has_right)
        def _():
            gather_copy(mine, o, phase, 1).start()

        @pl.when(has_left)
        def _():
            gather_copy(mine, o, phase, 0).start()

    slot_copy = pltpu.make_async_copy(slot_map, slot_of, slot_sem)
    slot_copy.start()

    def place(position, carry):
        value = tiles[slot_of[lax.div(position, lanes), lax.rem(position, lanes)]]
        rounded = value.astype(jnp.bfloat16)
        at_row = pl.multiple_of(lax.div(position, col_tiles) * tile, tile)
        at_col = pl.multiple_of(lax.rem(position, col_tiles) * tile, tile)
        high[pl.ds(at_row, tile), pl.ds(at_col, tile)] = rounded
        low[pl.ds(at_row, tile), pl.ds(at_col, tile)] = (
            value - rounded.astype(jnp.float32)
        ).astype(jnp.bfloat16)
        return carry

    def relay(phase, distance):
        @pl.when(o >= distance)
        def _():
            which = o - distance
            gather_copy(held(which, phase), which, phase, 1).wait_recv()

            @pl.when(has_right)
            def _():
                gather_copy(held(which, phase), which, phase, 1).start()

        @pl.when(o + distance < no)
        def _():
            which = o + distance
            gather_copy(held(which, phase), which, phase, 0).wait_recv()

            @pl.when(has_left)
            def _():
                gather_copy(held(which, phase), which, phase, 0).start()

    chunk = width // CHUNKS

    def split(phase):
        for side in range(2):
            value = amp[:, :, side, phase].reshape(half, depth)
            rounded = value.astype(jnp.bfloat16)
            lhs[phase, pl.ds(side * half, half)] = rounded
            lhs[phase, pl.ds(rows + side * half, half)] = (
                value - rounded.astype(jnp.float32)
            ).astype(jnp.bfloat16)

    def core_copy(phase, at):
        cols = pl.ds(at * chunk, chunk)
        return pltpu.make_async_remote_copy(
            src_ref=part.at[phase, 1 - core, :, cols],
            dst_ref=partner_part.at[phase, :, cols],
            send_sem=core_send.at[phase, at],
            recv_sem=core_recv.at[phase, at],
            device_id=other_core,
            device_id_type=MESH,
        )

    def chip_copy(phase, mask, at):
        cols = pl.ds(at * chunk, chunk)
        there = flip(chip, mask, chips)
        return pltpu.make_async_remote_copy(
            src_ref=summed.at[phase, there, :, cols],
            dst_ref=arrived.at[phase, mask - 1, :, cols],
            send_sem=chip_send.at[phase, mask - 1, at],
            recv_sem=chip_recv.at[phase, mask - 1, at],
            device_id=(o, 2 * there + core),
            device_id_type=MESH,
        )

    def multiply(phase, at):
        cols = pl.ds(at * chunk, chunk)
        wide = jnp.dot(lhs[phase], high[:, cols], preferred_element_type=jnp.float32)
        narrow = jnp.dot(
            lhs[phase, pl.ds(0, rows)], low[:, cols], preferred_element_type=jnp.float32
        )
        total = wide[:rows] + (wide[rows:] + narrow)
        part[phase, :, :, cols] = total.reshape(2, half, chunk)
        core_copy(phase, at).start()

    def pass_on(phase, at):
        cols = pl.ds(at * chunk, chunk)
        core_copy(phase, at).wait_recv()
        total = part[phase, core, :, cols] + partner_part[phase, :, cols]
        summed[phase, :, :, cols] = total.reshape(chips, level, chunk)
        for mask in range(chips - 1, 0, -1):
            chip_copy(phase, mask, at).start()

    tile_copy.wait()
    slot_copy.wait()
    own_copy.wait()
    far = jnp.maximum(o, no - 1 - o)
    parts = max(no // 2, 1)

    def round_of(distance, carry):
        first = lax.div(positions * (distance - 1), parts)
        last = lax.div(positions * distance, parts)
        lax.fori_loop(
            jnp.minimum(first, positions), jnp.minimum(last, positions), place, 0
        )
        relay(0, distance)

        @pl.when(distance == far)
        def _():
            split(0)
            for at in range(CHUNKS):
                multiply(0, at)

        relay(1, distance)
        return carry

    lax.fori_loop(1, no, round_of, 0)
    for at in range(CHUNKS):
        pass_on(0, at)
    split(1)
    for at in range(CHUNKS):
        multiply(1, at)
    for at in range(CHUNKS):
        pass_on(1, at)

    small[2].wait()
    small[3].wait()
    shape = (level, chunk)
    row_index = lax.broadcasted_iota(jnp.int32, shape, 0)
    for phase in range(PHASES):
        energy = jnp.zeros(shape, jnp.float32)
        for row in range(level):
            energy = jnp.where(row_index == row, occ_energy[phase * level + row], energy)
        for at in range(CHUNKS):
            cols = pl.ds(at * chunk, chunk)
            total = summed[phase, chip, :, cols]
            for mask in range(1, chips):
                chip_copy(phase, mask, at).wait_recv()
                total = total + arrived[phase, mask - 1, :, cols]
            out_ref[pl.ds(phase * level, level), cols] = total / (virt_energy[:, cols] - energy)

    for phase in range(PHASES):
        for at in range(CHUNKS):
            core_copy(phase, at).wait_send()
            for mask in range(1, chips):
                chip_copy(phase, mask, at).wait_send()
        for which in range(no):

            @pl.when(has_right & (o >= which))
            def _():
                gather_copy(held(which, phase), which, phase, 1).wait_send()

            @pl.when(has_left & (o <= which))
            def _():
                gather_copy(held(which, phase), which, phase, 0).wait_send()


def body(no, nv, amplitudes, tiles, tile_code, tile_count, occ_energy, virt_energy):
    block, depth = amplitudes.shape
    slots, tile, _ = tiles.shape
    width = virt_energy.shape[0]
    dest = occ_energy.shape[0]
    chips = nv // 2
    level = dest // PHASES
    pairs = block // (2 * dest)
    rows = block * no // PHASES
    map_shape = (max(8, (depth // tile) * (width // tile) // 128), 128)
    f32, bf16, i32 = jnp.float32, jnp.bfloat16, jnp.int32
    vmem, smem, dma = pltpu.VMEM, pltpu.SMEM, pltpu.SemaphoreType.DMA
    return pl.pallas_call(
        functools.partial(kernel, no, nv),
        out_shape=jax.ShapeDtypeStruct((dest, width), f32),
        in_specs=[pl.BlockSpec(memory_space=pltpu.HBM)] * 6,
        out_specs=pl.BlockSpec(memory_space=pltpu.VMEM),
        scratch_shapes=[
            smem(tile_code.shape, i32),
            smem(tile_count.shape, i32),
            smem((dest,), f32),
            vmem((1, width), f32),
            vmem(map_shape, i32),
            smem(map_shape, i32),
            vmem((slots + 1, tile, tile), f32),
            vmem((depth, width), bf16),
            vmem((depth, width), bf16),
            vmem((no, pairs, 2, PHASES, level, depth), f32),
            vmem((PHASES, 2 * rows, depth), bf16),
            vmem((PHASES, 2, rows // 2, width), f32),
            vmem((PHASES, rows // 2, width), f32),
            vmem((PHASES, chips, level, width), f32),
            vmem((PHASES, chips - 1, level, width), f32),
            dma((4,)),
            dma,
            dma,
            dma,
            dma((2, no, PHASES)),
            dma((no, PHASES)),
            dma((PHASES, CHUNKS)),
            dma((PHASES, CHUNKS)),
            dma((PHASES, chips - 1, CHUNKS)),
            dma((PHASES, chips - 1, CHUNKS)),
        ],
        compiler_params=pltpu.CompilerParams(
            collective_id=0, has_side_effects=True, vmem_limit_bytes=GRANT
        ),
    )(
        *(
            a if a is tile_count else pltpu.with_memory_space_constraint(a, pltpu.HBM)
            for a in (
                tile_code,
                tile_count,
                occ_energy,
                virt_energy.reshape(1, width),
                amplitudes.reshape(pairs, 2, PHASES, level, depth),
                tiles,
            )
        )
    )


def solution(mesh):
    placed = (
        P("occ", "virt"),
        P(("occ", "virt"), None, None),
        P(("occ", "virt")),
        P(("occ", "virt")),
        P("virt"),
        P("occ"),
    )
    return jax.shard_map(
        functools.partial(body, mesh.shape["occ"], mesh.shape["virt"]),
        mesh=mesh, in_specs=placed, out_specs=P("virt", "occ"), check_vma=False,
    )
```

```python
import functools

import jax
import jax.numpy as jnp
from jax import lax
from jax.experimental import pallas as pl
from jax.experimental.pallas import tpu as pltpu
from jax.sharding import PartitionSpec as P

MESH = pl.DeviceIdType.MESH
PHASES = 2
CHUNKS = 4
GRANT = 50 * 2**20


def flip(index, mask, size):
    out = index * 0
    bit = 1
    while bit < size:
        digit = lax.rem(lax.div(index, bit), 2)
        if mask & bit:
            digit = 1 - digit
        out = out + digit * bit
        bit *= 2
    return out


def kernel(
    no, nv,
    code_in, count_in, occ_in, virt_in, amp_in, tiles_in, out_ref,
    code, count, occ_energy, virt_energy, slot_map, slot_of,
    tiles, high, low, amp, lhs, part, partner_part, summed, arrived,
    small_sem, slot_sem, tile_sem, own_sem,
    gather_send, gather_recv, core_send, core_recv, chip_send, chip_recv,
):
    o = lax.axis_index("occ")
    v = lax.axis_index("virt")
    core = lax.rem(v, 2)
    chip = lax.div(v, 2)
    chips = nv // 2
    depth = amp_in.shape[-1]
    tile = tiles_in.shape[1]
    dest, width = out_ref.shape
    level = dest // PHASES
    rows = lhs.shape[1] // 2
    half = rows // 2
    col_tiles = width // tile
    positions = (depth // tile) * col_tiles
    slots = tiles_in.shape[0]

    small = [
        pltpu.make_async_copy(source, target, small_sem.at[number])
        for number, (source, target) in enumerate(
            ((code_in, code), (count_in, count), (occ_in, occ_energy), (virt_in, virt_energy))
        )
    ]
    small[0].start()
    small[1].start()
    own_copy = pltpu.make_async_copy(amp_in, amp.at[o], own_sem)
    own_copy.start()
    tile_copy = pltpu.make_async_copy(tiles_in, tiles.at[pl.ds(0, slots)], tile_sem)
    tile_copy.start()
    small[2].start()
    small[3].start()
    has_left = o > 0
    has_right = o < no - 1
    other_core = (o, v + 1 - 2 * core)

    barrier = pltpu.get_barrier_semaphore()

    @pl.when(has_left)
    def _():
        pl.semaphore_signal(barrier, inc=1, device_id=(o - 1, v), device_id_type=MESH)

    @pl.when(has_right)
    def _():
        pl.semaphore_signal(barrier, inc=1, device_id=(o + 1, v), device_id_type=MESH)

    for mask in range(chips - 1, 0, -1):
        there = flip(chip, mask, chips)
        pl.semaphore_signal(barrier, inc=1, device_id=(o, 2 * there + core), device_id_type=MESH)
    pl.semaphore_signal(barrier, inc=1, device_id=other_core, device_id_type=MESH)

    pl.semaphore_wait(barrier, chips + has_left.astype(jnp.int32) + has_right.astype(jnp.int32))

    def gather_copy(source, which, phase, side):
        return pltpu.make_async_remote_copy(
            src_ref=source,
            dst_ref=amp.at[which, :, :, phase],
            send_sem=gather_send.at[side, which, phase],
            recv_sem=gather_recv.at[which, phase],
            device_id=(o + 2 * side - 1, v),
            device_id_type=MESH,
        )

    def held(which, phase):
        return amp.at[which, :, :, phase]

    for phase in range(PHASES):
        mine = amp_in.at[:, :, phase]

        @pl.when(has_right)
        def _():
            gather_copy(mine, o, phase, 1).start()

        @pl.when(has_left)
        def _():
            gather_copy(mine, o, phase, 0).start()

    small[0].wait()
    small[1].wait()
    lanes = slot_map.shape[1]
    place_index = lax.broadcasted_iota(jnp.int32, slot_map.shape, 0) * lanes + (
        lax.broadcasted_iota(jnp.int32, slot_map.shape, 1)
    )
    found = jnp.full(slot_map.shape, slots, jnp.int32)
    live = count[0]
    for slot in range(slots):
        found = jnp.where(place_index == jnp.where(slot < live, code[slot], -1), slot, found)
    slot_map[...] = found
    own_copy.wait()
    tile_copy.wait()
    tiles[slots] = jnp.zeros(tiles.shape[1:], tiles.dtype)
    slot_copy = pltpu.make_async_copy(slot_map, slot_of, slot_sem)
    slot_copy.start()

    def place(position, carry):
        value = tiles[slot_of[lax.div(position, lanes), lax.rem(position, lanes)]]
        rounded = value.astype(jnp.bfloat16)
        at_row = pl.multiple_of(lax.div(position, col_tiles) * tile, tile)
        at_col = pl.multiple_of(lax.rem(position, col_tiles) * tile, tile)
        high[pl.ds(at_row, tile), pl.ds(at_col, tile)] = rounded
        low[pl.ds(at_row, tile), pl.ds(at_col, tile)] = (
            value - rounded.astype(jnp.float32)
        ).astype(jnp.bfloat16)
        return carry

    def relay(phase, distance):
        @pl.when(o >= distance)
        def _():
            which = o - distance
            gather_copy(held(which, phase), which, phase, 1).wait_recv()

            @pl.when(has_right)
            def _():
                gather_copy(held(which, phase), which, phase, 1).start()

        @pl.when(o + distance < no)
        def _():
            which = o + distance
            gather_copy(held(which, phase), which, phase, 0).wait_recv()

            @pl.when(has_left)
            def _():
                gather_copy(held(which, phase), which, phase, 0).start()

    chunk = width // CHUNKS

    def split(phase):
        for side in range(2):
            value = amp[:, :, side, phase].reshape(half, depth)
            rounded = value.astype(jnp.bfloat16)
            lhs[phase, pl.ds(side * half, half)] = rounded
            lhs[phase, pl.ds(rows + side * half, half)] = (
                value - rounded.astype(jnp.float32)
            ).astype(jnp.bfloat16)

    def core_copy(phase, at):
        cols = pl.ds(at * chunk, chunk)
        return pltpu.make_async_remote_copy(
            src_ref=part.at[phase, 1 - core, :, cols],
            dst_ref=partner_part.at[phase, :, cols],
            send_sem=core_send.at[phase, at],
            recv_sem=core_recv.at[phase, at],
            device_id=other_core,
            device_id_type=MESH,
        )

    def chip_copy(phase, mask, at):
        cols = pl.ds(at * chunk, chunk)
        there = flip(chip, mask, chips)
        return pltpu.make_async_remote_copy(
            src_ref=summed.at[phase, there, :, cols],
            dst_ref=arrived.at[phase, mask - 1, :, cols],
            send_sem=chip_send.at[phase, mask - 1, at],
            recv_sem=chip_recv.at[phase, mask - 1, at],
            device_id=(o, 2 * there + core),
            device_id_type=MESH,
        )

    def multiply(phase, at):
        cols = pl.ds(at * chunk, chunk)
        wide = jnp.dot(lhs[phase], high[:, cols], preferred_element_type=jnp.float32)
        narrow = jnp.dot(
            lhs[phase, pl.ds(0, rows)], low[:, cols], preferred_element_type=jnp.float32
        )
        total = wide[:rows] + (wide[rows:] + narrow)
        part[phase, :, :, cols] = total.reshape(2, half, chunk)
        core_copy(phase, at).start()

    def pass_on(phase, at):
        cols = pl.ds(at * chunk, chunk)
        core_copy(phase, at).wait_recv()
        total = part[phase, core, :, cols] + partner_part[phase, :, cols]
        summed[phase, :, :, cols] = total.reshape(chips, level, chunk)
        for mask in range(chips - 1, 0, -1):
            chip_copy(phase, mask, at).start()

    slot_copy.wait()
    far = jnp.maximum(o, no - 1 - o)
    parts = max(no // 2, 1)

    def round_of(distance, carry):
        first = lax.div(positions * (distance - 1), parts)
        last = lax.div(positions * distance, parts)
        lax.fori_loop(
            jnp.minimum(first, positions), jnp.minimum(last, positions), place, 0
        )
        relay(0, distance)

        @pl.when(distance == far)
        def _():
            split(0)
            for at in range(CHUNKS):
                multiply(0, at)

        relay(1, distance)
        return carry

    lax.fori_loop(1, no, round_of, 0)
    for at in range(CHUNKS):
        pass_on(0, at)
    split(1)
    for at in range(CHUNKS):
        multiply(1, at)
    for at in range(CHUNKS):
        pass_on(1, at)

    small[2].wait()
    small[3].wait()
    shape = (level, chunk)
    row_index = lax.broadcasted_iota(jnp.int32, shape, 0)
    for phase in range(PHASES):
        energy = jnp.zeros(shape, jnp.float32)
        for row in range(level):
            energy = jnp.where(row_index == row, occ_energy[phase * level + row], energy)
        for at in range(CHUNKS):
            cols = pl.ds(at * chunk, chunk)
            total = summed[phase, chip, :, cols]
            for mask in range(1, chips):
                chip_copy(phase, mask, at).wait_recv()
                total = total + arrived[phase, mask - 1, :, cols]
            out_ref[pl.ds(phase * level, level), cols] = total / (virt_energy[:, cols] - energy)

    for phase in range(PHASES):
        for at in range(CHUNKS):
            core_copy(phase, at).wait_send()
            for mask in range(1, chips):
                chip_copy(phase, mask, at).wait_send()
        for which in range(no):

            @pl.when(has_right & (o >= which))
            def _():
                gather_copy(held(which, phase), which, phase, 1).wait_send()

            @pl.when(has_left & (o <= which))
            def _():
                gather_copy(held(which, phase), which, phase, 0).wait_send()


def body(no, nv, amplitudes, tiles, tile_code, tile_count, occ_energy, virt_energy):
    block, depth = amplitudes.shape
    slots, tile, _ = tiles.shape
    width = virt_energy.shape[0]
    dest = occ_energy.shape[0]
    chips = nv // 2
    level = dest // PHASES
    pairs = block // (2 * dest)
    rows = block * no // PHASES
    map_shape = (max(8, (depth // tile) * (width // tile) // 128), 128)
    f32, bf16, i32 = jnp.float32, jnp.bfloat16, jnp.int32
    vmem, smem, dma = pltpu.VMEM, pltpu.SMEM, pltpu.SemaphoreType.DMA
    return pl.pallas_call(
        functools.partial(kernel, no, nv),
        out_shape=jax.ShapeDtypeStruct((dest, width), f32),
        in_specs=[pl.BlockSpec(memory_space=pltpu.HBM)] * 6,
        out_specs=pl.BlockSpec(memory_space=pltpu.VMEM),
        scratch_shapes=[
            smem(tile_code.shape, i32),
            smem(tile_count.shape, i32),
            smem((dest,), f32),
            vmem((1, width), f32),
            vmem(map_shape, i32),
            smem(map_shape, i32),
            vmem((slots + 1, tile, tile), f32),
            vmem((depth, width), bf16),
            vmem((depth, width), bf16),
            vmem((no, pairs, 2, PHASES, level, depth), f32),
            vmem((PHASES, 2 * rows, depth), bf16),
            vmem((PHASES, 2, rows // 2, width), f32),
            vmem((PHASES, rows // 2, width), f32),
            vmem((PHASES, chips, level, width), f32),
            vmem((PHASES, chips - 1, level, width), f32),
            dma((4,)),
            dma,
            dma,
            dma,
            dma((2, no, PHASES)),
            dma((no, PHASES)),
            dma((PHASES, CHUNKS)),
            dma((PHASES, CHUNKS)),
            dma((PHASES, chips - 1, CHUNKS)),
            dma((PHASES, chips - 1, CHUNKS)),
        ],
        compiler_params=pltpu.CompilerParams(
            collective_id=0, has_side_effects=True, vmem_limit_bytes=GRANT
        ),
    )(
        *(
            a if a is tile_count else pltpu.with_memory_space_constraint(a, pltpu.HBM)
            for a in (
                tile_code,
                tile_count,
                occ_energy,
                virt_energy.reshape(1, width),
                amplitudes.reshape(pairs, 2, PHASES, level, depth),
                tiles,
            )
        )
    )


def solution(mesh):
    placed = (
        P("occ", "virt"),
        P(("occ", "virt"), None, None),
        P(("occ", "virt")),
        P(("occ", "virt")),
        P("virt"),
        P("occ"),
    )
    return jax.shard_map(
        functools.partial(body, mesh.shape["occ"], mesh.shape["virt"]),
        mesh=mesh, in_specs=placed, out_specs=P("virt", "occ"), check_vma=False,
    )
```
